32 devices in a mesh: group: 2 (over x), depth: 2 (over core), col: 8 (over z, y).
Axes of the slice: x: 2, y: 2, z: 4, core: 2. Of those that a mesh axis runs over, the one named last changes fastest.
Arguments:
- alignment_activations: bfloat16 [256, 32, 256], P(('group', 'depth'), 'col'), parts along dimension 0, may hold values from -8 to 8
- alignment_mask: int32 [256, 32], P(('group', 'depth'), 'col'), parts along dimension 0, may hold values from 0 to 1, as said below
- pair_activation_input: bfloat16 [64, 32, 128], P(('group', 'col'), 'depth'), parts along dimension 0, may hold values from -6 to 6
- pair_update_mask: int32 [64, 32], P(('group', 'col'), 'depth'), parts along dimension 0, may hold values 0 or 1
- pair_output_gradient: bfloat16 [64, 32, 128], P(('group', 'col'), 'depth'), parts along dimension 0, may hold values from -6 to 6
- layer_scale_factor: float32 [256], replicated, may hold values from 0.25 to 1.75
- first_projector: bfloat16 [256, 32], replicated, may hold values from -0.375 to 0.375
- second_projector: bfloat16 [256, 32], replicated, may hold values from -0.375 to 0.375
- output_weight: bfloat16 [1024, 128], replicated, may hold values from -1.5 to 1.5
- pair_norm_gain: float32 [128], replicated, may hold values from 0.25 to 1.75
- hidden_weight: bfloat16 [128, 512], replicated, may hold values from -0.5 to 0.5
- back_weight: bfloat16 [512, 128], replicated, may hold values from -0.25 to 0.25
Outputs:
- features_derivative: bfloat16 [256, 32, 256], P(('group', 'depth'), 'col'), parts along dimension 0
- couple_features_derivative: bfloat16 [64, 32, 128], P(('group', 'col'), 'depth'), parts along dimension 0
- first_projector_derivative: float32 [512, 32], P('group'), parts along dimension 0
- second_projector_derivative: float32 [512, 32], P('group'), parts along dimension 0
- result_matrix_derivative: float32 [2048, 128], P('group'), parts along dimension 0
- middle_matrix_derivative: float32 [256, 512], P('group'), parts along dimension 0
- final_matrix_derivative: float32 [1024, 128], P('group'), parts along dimension 0
The draws below stay inside these ranges and needn't reach their ends.
There are 2 independent parts, one for each index of `group`. The reference program is written for one: setup_inputs(seed, part) draws one part's arguments, and reference() takes and returns one part's arrays. A program takes and returns all parts, laid end to end along the dimension named above; an argument that names none is the same for every part. Nothing has to cross between parts.
Inputs may be any that keep to these rules, and one draw needn't show every extreme that they name: `alignment_mask`: sequence 0 is present at every residue.
All inputs are finite; a program needn't handle non-finite values. No bound on the sum of `pair_update_mask` on one device may be relied on, other than what follows from the above.
Results may differ from the reference program's by a relative error of at most 0.014.
Values may be sent and summed in bfloat16 or wider, within the bound.
A program may use at most 64 MiB of HBM per device.

```python
import jax
import jax.numpy as jnp
from jax import lax

FEATURE_COUNT = 256
PROJECTOR_WIDTH = 32
CZ = 128
HID = 512
RES_DEV = 4
ALIGNED_COUNT = 128
CROP_LENGTH = 32
OUTER = 1024
N_COL = 8


def draw_alignment_activations(key, part):
    random_seed_factor, random_seed_start = jax.random.split(key, 2)
    feature_factor = jnp.exp(jax.random.uniform(random_seed_factor, (FEATURE_COUNT,), jnp.float32, -1.2, 1.2))
    entries_drawn = jax.random.normal(random_seed_start, (ALIGNED_COUNT, CROP_LENGTH, FEATURE_COUNT), jnp.float32) * feature_factor
    return jnp.clip(entries_drawn, -8.0, 8.0).astype(jnp.bfloat16)


def draw_alignment_mask(key, part):
    seq_index = jnp.arange(ALIGNED_COUNT, dtype=jnp.int32)
    limits = 150 + 800 * seq_index // ALIGNED_COUNT
    tickets = jax.random.randint(key, (ALIGNED_COUNT, CROP_LENGTH), 0, 1000, dtype=jnp.int32)
    present = (tickets < limits[:, None]).astype(jnp.int32)
    return present.at[0].set(1)


def touch_ends(array, rng, smallest, top_value):
    spot = [jax.random.randint(jax.random.fold_in(rng, axis), (), 0, length) for axis, length in enumerate(array.shape)]
    widest = array.shape.index(max(array.shape))
    neighbour = spot[:widest] + [(spot[widest] + 1) % array.shape[widest]] + spot[widest + 1:]
    return array.at[tuple(spot)].set(smallest).at[tuple(neighbour)].set(top_value)


def block_scale(stream_key, shape, cuts, smallest, largest):
    level = 1.0
    for axis_at, parts in cuts:
        steps = jax.random.uniform(jax.random.fold_in(jax.random.fold_in(stream_key, 6), axis_at), (parts,), jnp.float32, smallest / len(cuts), largest / len(cuts))
        level = level * jnp.repeat(jnp.exp(steps), shape[axis_at] // parts).reshape((-1,) + (1,) * (len(shape) - 1 - axis_at))
    return level


def gaussian(key, dims, width, reach, cuts=(), held_as=jnp.bfloat16):
    gain = block_scale(key, dims, cuts, -0.22, 0.18) if cuts else 1.0
    entries = jax.random.normal(key, dims, jnp.float32) * width * gain
    return jnp.minimum(jnp.maximum(entries, -reach), reach).astype(held_as)


def setup_inputs(seed: int = 0, part: int = 0) -> dict:
    splits = jax.random.split(jax.random.key(seed), 13)
    part_keys = jax.random.split(jax.random.fold_in(splits[12], part), 13)
    alignment_activations = draw_alignment_activations(jax.random.fold_in(jax.random.fold_in(splits[12], part), 71), part)
    alignment_mask = draw_alignment_mask(jax.random.fold_in(jax.random.fold_in(splits[12], part), 71), part)
    pair_activation_input = gaussian(part_keys[2], (CROP_LENGTH, CROP_LENGTH, CZ), 1.0, 6.0, ((0, 8), (1, 2)))
    pair_update_mask = touch_ends((jax.random.randint(part_keys[3], (CROP_LENGTH, CROP_LENGTH), 0, 8) < 7).astype(jnp.int32), jax.random.fold_in(part_keys[3], 1), 0, 1)
    pair_output_gradient = gaussian(part_keys[4], (CROP_LENGTH, CROP_LENGTH, CZ), 1.0, 6.0, ((0, 8), (1, 2)))
    layer_scale_factor = jnp.clip(1.0 + 0.15 * jax.random.normal(splits[5], (FEATURE_COUNT,), jnp.float32), 0.25, 1.75)
    first_projector = gaussian(splits[6], (FEATURE_COUNT, PROJECTOR_WIDTH), FEATURE_COUNT ** -0.5, 0.375)
    second_projector = gaussian(splits[7], (FEATURE_COUNT, PROJECTOR_WIDTH), FEATURE_COUNT ** -0.5, 0.375)
    output_weight = gaussian(splits[8], (OUTER, CZ), 16 ** -0.5, 1.5)
    pair_norm_gain = jnp.clip(1.0 + 0.15 * jax.random.normal(splits[9], (CZ,), jnp.float32), 0.25, 1.75)
    hidden_weight = gaussian(splits[10], (CZ, HID), CZ ** -0.5, 0.5)
    back_weight = gaussian(splits[11], (HID, CZ), HID ** -0.5, 0.25)
    return dict(alignment_activations=alignment_activations, alignment_mask=alignment_mask, pair_activation_input=pair_activation_input, pair_update_mask=pair_update_mask, pair_output_gradient=pair_output_gradient, layer_scale_factor=layer_scale_factor, first_projector=first_projector, second_projector=second_projector, output_weight=output_weight, pair_norm_gain=pair_norm_gain, hidden_weight=hidden_weight, back_weight=back_weight)


epsilon = 1e-05
highest = lax.Precision.HIGHEST

def norm_pieces(entries_drawn):
    center = entries_drawn - lax.optimization_barrier(jnp.mean(entries_drawn, axis=-1, keepdims=True))
    inv_std = lax.rsqrt(lax.optimization_barrier(jnp.mean(center * center, axis=-1, keepdims=True)) + epsilon)
    return (center * inv_std, inv_std)

def standardize_adjoint(grad_scaled, scaled, inv_std):
    mean_grad = lax.optimization_barrier(jnp.mean(grad_scaled, axis=-1, keepdims=True))
    mean_cross = lax.optimization_barrier(jnp.mean(grad_scaled * scaled, axis=-1, keepdims=True))
    return inv_std * (grad_scaled - mean_grad - scaled * mean_cross)

def silu_pieces(pre_act):
    sigma = jax.nn.sigmoid(pre_act)
    return (pre_act * sigma, sigma * (1.0 + pre_act * (1.0 - sigma)))

def return_journey(entries_drawn):
    return lax.optimization_barrier(entries_drawn.astype(jnp.bfloat16)).astype(jnp.float32)

def reference(alignment_activations, alignment_mask, pair_activation_input, pair_update_mask, pair_output_gradient, layer_scale_factor, first_projector, second_projector, output_weight, pair_norm_gain, hidden_weight, back_weight):
    standardized_features, reciprocal_spread = norm_pieces(alignment_activations.astype(jnp.float32))
    normalized_broad = return_journey(standardized_features * layer_scale_factor)
    mask_unconverted = alignment_mask.astype(jnp.float32)
    mask_floating = mask_unconverted[:, :, None]
    left_wide = return_journey(jnp.einsum('src,ck->srk', normalized_broad, first_projector.astype(jnp.float32)) * mask_floating)
    right_wide = return_journey(jnp.einsum('src,ck->srk', normalized_broad, second_projector.astype(jnp.float32)) * mask_floating)
    out_wide = output_weight.astype(jnp.float32)
    starts = jnp.arange(N_COL, dtype=jnp.int32) * RES_DEV

    def row_block(acc_state, start_row):
        grad_right, grad_out, grad_hid, grad_bk = acc_state
        left_rows = lax.dynamic_slice_in_dim(left_wide, start_row, RES_DEV, 1)
        mask_rows = lax.dynamic_slice_in_dim(mask_unconverted, start_row, RES_DEV, 1)
        act_rows = lax.dynamic_slice_in_dim(pair_activation_input, start_row, RES_DEV, 0).astype(jnp.float32)
        grad_rows = lax.dynamic_slice_in_dim(pair_output_gradient, start_row, RES_DEV, 0)
        pmask_rows = lax.dynamic_slice_in_dim(pair_update_mask, start_row, RES_DEV, 0)
        outer_sum = jnp.einsum('sic,sjd->ijcd', left_rows, right_wide).reshape(RES_DEV * CROP_LENGTH, OUTER)
        pair_count = jnp.einsum('si,sj->ij', mask_rows, mask_unconverted).reshape(RES_DEV * CROP_LENGTH, 1)
        projected = jnp.dot(outer_sum, out_wide, precision=highest)
        mid_act = act_rows.reshape(RES_DEV * CROP_LENGTH, CZ) + projected / pair_count
        pair_scaled, pair_inv = norm_pieces(mid_act)
        pair_normed = (pair_scaled * pair_norm_gain).astype(jnp.bfloat16)
        pre_act = jnp.dot(pair_normed, hidden_weight, preferred_element_type=jnp.float32)
        act_value, act_slope = silu_pieces(pre_act)
        hidden = act_value.astype(jnp.bfloat16)
        masked_grad = (grad_rows * pmask_rows.astype(jnp.bfloat16)[:, :, None]).reshape(RES_DEV * CROP_LENGTH, CZ)
        grad_bk = grad_bk + jnp.dot(hidden.T, masked_grad, preferred_element_type=jnp.float32)
        back_prod = jnp.dot(masked_grad, back_weight.T, preferred_element_type=jnp.float32)
        grad_hidden = (back_prod * act_slope).astype(jnp.bfloat16)
        grad_hid = grad_hid + jnp.dot(pair_normed.T, grad_hidden, preferred_element_type=jnp.float32)
        grad_scaled = jnp.dot(grad_hidden, hidden_weight.T, preferred_element_type=jnp.float32) * pair_norm_gain
        grad_mid = grad_rows.reshape(RES_DEV * CROP_LENGTH, CZ).astype(jnp.float32) + standardize_adjoint(grad_scaled, pair_scaled, pair_inv)
        grad_opm = (grad_mid / pair_count).astype(jnp.bfloat16)
        grad_out = grad_out + jnp.dot(outer_sum.T, grad_opm.astype(jnp.float32), precision=highest)
        grad_outer = return_journey(jnp.dot(grad_opm, output_weight.T, preferred_element_type=jnp.float32)).reshape(RES_DEV, CROP_LENGTH, PROJECTOR_WIDTH, PROJECTOR_WIDTH)
        grad_left_rows = jnp.einsum('ijcd,sjd->sic', grad_outer, right_wide)
        grad_right = grad_right + jnp.einsum('ijcd,sic->sjd', grad_outer, left_rows)
        pair_rows = grad_mid.astype(jnp.bfloat16).reshape(RES_DEV, CROP_LENGTH, CZ)
        return ((grad_right, grad_out, grad_hid, grad_bk), (pair_rows, grad_left_rows))
    init_state = (jnp.zeros((ALIGNED_COUNT, CROP_LENGTH, PROJECTOR_WIDTH), jnp.float32), jnp.zeros((OUTER, CZ), jnp.float32), jnp.zeros((CZ, HID), jnp.float32), jnp.zeros((HID, CZ), jnp.float32))
    final_state, (pair_blocks, left_blocks) = lax.scan(row_block, init_state, starts)
    grad_right_acc, result_matrix_derivative, middle_matrix_derivative, final_matrix_derivative = final_state
    couple_features_derivative = pair_blocks.reshape(CROP_LENGTH, CROP_LENGTH, CZ)
    grad_left_acc = jnp.transpose(left_blocks, (1, 0, 2, 3)).reshape(ALIGNED_COUNT, CROP_LENGTH, PROJECTOR_WIDTH)
    grad_left = return_journey(grad_left_acc * mask_floating)
    grad_right = return_journey(grad_right_acc * mask_floating)
    first_projector_derivative = jnp.einsum('src,srk->ck', normalized_broad, grad_left)
    second_projector_derivative = jnp.einsum('src,srk->ck', normalized_broad, grad_right)
    standardized_derivative = jnp.einsum('srk,ck->src', grad_left, first_projector.astype(jnp.float32))
    standardized_derivative = standardized_derivative + jnp.einsum('srk,ck->src', grad_right, second_projector.astype(jnp.float32))
    features_derivative = standardize_adjoint(standardized_derivative * layer_scale_factor, standardized_features, reciprocal_spread).astype(jnp.bfloat16)
    return (features_derivative, couple_features_derivative, first_projector_derivative, second_projector_derivative, result_matrix_derivative, middle_matrix_derivative, final_matrix_derivative)
```

```python
import functools

import jax
import jax.numpy as jnp
from jax import lax
from jax.experimental import pallas as pl
from jax.experimental.pallas import tpu as pltpu
from jax.sharding import PartitionSpec as P

EPS = 1e-05
F32 = jnp.float32
BF16 = jnp.bfloat16
MESH = pl.DeviceIdType.MESH


def mm(a, b, ca=1, cb=0):
    return lax.dot_general(a, b, (((ca,), (cb,)), ((), ())), preferred_element_type=F32)


def norm_pieces(v):
    center = v - jnp.mean(v, axis=-1, keepdims=True)
    inv = lax.rsqrt(jnp.mean(center * center, axis=-1, keepdims=True) + EPS)
    return center * inv, inv


def standardize_adjoint(g, scaled, inv):
    mean_g = jnp.mean(g, axis=-1, keepdims=True)
    mean_c = jnp.mean(g * scaled, axis=-1, keepdims=True)
    return inv * (g - mean_g - scaled * mean_c)


def iota(shape, axis):
    return lax.broadcasted_iota(jnp.int32, shape, axis)


def kernel(
    ncol, seqs, res, cols, cw,
    x_ref, am_ref, pin_ref, pm_ref, pg_ref, ls_ref, fp_ref, sp_ref, ow_ref, png_ref, hw_ref, bw_ref,
    feat_ref, couple_ref, wsum_ref, small_ref,
    lbuf, rbuf, mloc, mrow, mcol, lsend, rsend,
    outer, gbuf, scaled_sc, normed_sc,
    grsend, grrecv, glsend, glrecv,
    wb, w1recv, w1s, w2recv, w3, wout,
    sm, srecv, smine, sout,
    sem_l, sem_r, sem_ml, sem_mr, sem_gr, sem_gl, sem_w1, sem_w2, sem_w3, sem_w4, sem_s1, sem_s2,
    snd_l, snd_r, snd_ml, snd_mr, snd_gr, snd_gl, snd_w1, snd_w2, snd_w3, snd_w4, snd_s1, snd_s2,
):
    g = lax.axis_index("group")
    e = lax.axis_index("depth")
    k = lax.axis_index("col")
    f = 1 - e
    n = 2 * ncol
    me = e * ncol + k
    lanes = res * cw
    jts = cols // res
    grp = lanes // cw
    cts = cw // grp
    pairs = res * cols
    z = pin_ref.shape[1]

    barrier = pltpu.get_barrier_semaphore()
    for t in range(1, n):
        peer = lax.rem(me + t, n)
        pl.semaphore_signal(
            barrier, inc=1, device_id=(g, lax.div(peer, ncol), lax.rem(peer, ncol)),
            device_id_type=MESH,
        )

    def rcopy(src, dst, ssem, rsem, d, c):
        return pltpu.make_async_remote_copy(
            src_ref=src, dst_ref=dst, send_sem=ssem, recv_sem=rsem,
            device_id=(g, d, c), device_id_type=MESH,
        )

    scaled, inv = norm_pieces(x_ref[...].astype(F32))
    normed = (scaled * ls_ref[...]).astype(BF16)
    scaled_sc[...] = scaled
    normed_sc[...] = normed
    el_c = iota((cw, lanes), 0)
    el_l = iota((cw, lanes), 1)
    expand_l = (grp * lax.div(lax.rem(el_l, cw), res) + lax.div(el_l, cw) == el_c).astype(F32).astype(BF16)
    expand_r = (lax.rem(el_l, cw) == el_c).astype(F32).astype(BF16)
    wl = mm(fp_ref[...], expand_l).astype(BF16)
    wr = mm(sp_ref[...], expand_r).astype(BF16)
    pl_full = mm(normed, wl)
    pr_full = mm(normed, wr)
    ln = iota((seqs, lanes), 1)
    res_l = lax.rem(ln, res)
    res_r = lax.div(ln, cw)
    mask = am_ref[...].astype(F32)
    zero = jnp.zeros((seqs, lanes), F32)
    left, right, ml, mr, mpad = zero, zero, zero, zero, zero
    for r in range(res):
        col = jnp.broadcast_to(mask[:, r : r + 1], (seqs, lanes))
        left = jnp.where(res_l == r, pl_full[r * seqs : (r + 1) * seqs], left)
        right = jnp.where(res_r == r, pr_full[r * seqs : (r + 1) * seqs], right)
        ml = jnp.where(res_l == r, col, ml)
        mr = jnp.where(res_r == r, col, mr)
        mpad = jnp.where(ln == r, col, mpad)
    left = (left * ml).astype(BF16)
    right = (right * mr).astype(BF16)
    lsend[...] = left
    rsend[...] = right
    lbuf[e] = left
    eye = (iota((seqs, lanes), 0) == ln).astype(F32).astype(BF16)
    mt = mm(mpad.astype(BF16), eye, 0, 0)[0:8]
    mloc[...] = mt
    mrow[e] = mt
    own_e = lax.div(k, jts)
    own_jt = lax.rem(k, jts)

    pl.semaphore_wait(barrier, n - 1)

    c_left = rcopy(lsend, lbuf.at[e], snd_l, sem_l, f, k)
    c_ml = rcopy(mloc, mrow.at[e], snd_ml, sem_ml, f, k)

    def r_copies(t):
        kk = lax.rem(k + t, ncol)
        return (
            rcopy(rsend, rbuf.at[own_jt, e], snd_r.at[t], sem_r.at[own_jt, e], own_e, kk),
            rcopy(mloc, mcol.at[e, own_jt], snd_mr.at[t], sem_mr.at[own_jt, e], own_e, kk),
        )

    for t in range(1, ncol):
        for c in r_copies(t):
            c.start()

    @pl.when(own_e == e)
    def _():
        rbuf[own_jt, e] = right
        mcol[e, own_jt] = mt

    @pl.when(own_e != e)
    def _():
        for c in r_copies(0):
            c.start()

    c_left.start()
    c_ml.start()

    pgrad = pg_ref[...]
    sw_r = iota((pairs, pairs), 0)
    sw_c = iota((pairs, pairs), 1)
    swap = (lax.rem(sw_r, res) * cols + lax.div(sw_r, res) == sw_c).astype(F32).astype(BF16)
    pact = mm(swap, pin_ref[...])
    pgrad = mm(swap, pgrad)
    pick = (lax.rem(iota((pairs, res), 0), res) == iota((pairs, res), 1)).astype(F32).astype(BF16)
    prow = mm(pick, pm_ref[...].astype(F32).astype(BF16))
    pj_at = lax.div(iota((pairs, cols), 0), res) == iota((pairs, cols), 1)
    pcol = jnp.sum(jnp.where(pj_at, prow, 0.0), axis=1, keepdims=True)
    masked_grad = (pgrad * pcol).astype(BF16)
    back_prod = mm(masked_grad, bw_ref[...], 1, 1)

    c_left.wait()
    c_ml.wait()
    for jt in range(jts):
        for h in range(2):

            @pl.when(jnp.logical_or(own_e != e, jnp.logical_or(own_jt != jt, e != h)))
            def _():
                rcopy(rsend, rbuf.at[jt, h], snd_r.at[0], sem_r.at[jt, h], e, k).wait_recv()
                rcopy(mloc, mcol.at[h, jt], snd_mr.at[0], sem_mr.at[jt, h], e, k).wait_recv()

    pi = (lax.rem(iota((pairs, 8), 0), res) == iota((pairs, 8), 1)).astype(F32).astype(BF16)
    pj_r = lax.div(iota((pairs, jts * 8), 0), res)
    pj_l = iota((pairs, jts * 8), 1)
    pj = jnp.logical_and(
        lax.div(pj_r, res) == lax.div(pj_l, 8), lax.rem(pj_r, res) == lax.rem(pj_l, 8)
    ).astype(F32).astype(BF16)
    prod = jnp.zeros((pairs, lanes), F32)
    for h in range(2):
        mi = mm(pi, mrow[h].astype(BF16))
        mj = mm(pj, mcol[h].reshape(jts * 8, lanes).astype(BF16))
        prod = prod + mi * mj
    count = jnp.sum(prod, axis=1, keepdims=True)

    lall = lbuf[...].reshape(2 * seqs, lanes)
    atom = lax.div(iota((cw, lanes), 1), cw)
    top = lax.rem(iota((cw, lanes), 0), 2 * res) < res
    for jt in range(jts):
        o = mm(lall, rbuf[jt].reshape(2 * seqs, lanes), 0, 0)
        ts = []
        for q in range(grp):
            t_q = o[0:cw]
            if q:
                t_q = pltpu.roll(t_q, (cw * (0 - q)) % lanes, 1)
            for p in range(1, grp):
                v = o[p * cw : (p + 1) * cw]
                if p != q:
                    v = pltpu.roll(v, (cw * (p - q)) % lanes, 1)
                t_q = jnp.where(atom == p, v, t_q)
            ts.append(t_q)
        for q in range(0, grp, 2):
            even = jnp.where(top, ts[q], pltpu.roll(ts[q + 1], res, 0))
            odd = jnp.where(top, pltpu.roll(ts[q], cw - res, 0), ts[q + 1])
            at = (jt * res + q) * res
            for m in range(cts // 2):
                outer[2 * m, at : at + 2 * res, :] = even[m * 2 * res : (m + 1) * 2 * res]
                outer[2 * m + 1, at : at + 2 * res, :] = odd[m * 2 * res : (m + 1) * 2 * res]
    outer_b = jnp.concatenate([outer[ct].astype(BF16) for ct in range(cts)], axis=1)
    projected = mm(outer_b, ow_ref[...])

    mid_act = pact + projected / count
    pscaled, pinv = norm_pieces(mid_act)
    pnormed = (pscaled * png_ref[...]).astype(BF16)
    pre = mm(pnormed, hw_ref[...])
    sig = jax.nn.sigmoid(pre)
    hidden = (pre * sig).astype(BF16)
    grad_hidden = (back_prod * (sig * (1.0 + pre * (1.0 - sig)))).astype(BF16)
    gs = mm(grad_hidden, hw_ref[...], 1, 1) * png_ref[...]
    grad_mid = pgrad + standardize_adjoint(gs, pscaled, pinv)
    couple_ref[...] = mm(swap, grad_mid.astype(BF16), 0, 0).astype(BF16)
    opm = (grad_mid / count).astype(BF16)

    rows = wb.shape[2]
    g_out = mm(opm, ow_ref[...], 1, 1)
    tall = 2 * res
    perm_r = iota((cts * tall, cts * tall), 0)
    perm_c = iota((cts * tall, cts * tall), 1)
    perm_q = lax.div(perm_r, cw)
    perm_t = lax.div(lax.rem(perm_r, cw), res)
    perm = (perm_t * tall + perm_q * res + lax.rem(perm_r, res) == perm_c).astype(F32).astype(BF16)
    stack = jnp.concatenate(
        [
            jnp.concatenate(
                [
                    g_out[b * tall : (b + 1) * tall, ct * lanes : (ct + 1) * lanes]
                    for b in range(pairs // tall)
                ],
                axis=1,
            )
            for ct in range(cts)
        ],
        axis=0,
    )
    moved = mm(perm, stack.astype(BF16))
    gl = jnp.zeros((2 * seqs, lanes), F32)
    for jt in range(jts):
        us = []
        gps = []
        for q in range(grp):
            b = jt * (grp // 2) + q // 2
            us.append(moved[(q % 2) * cw : (q % 2 + 1) * cw, b * lanes : (b + 1) * lanes])
        for p in range(grp):
            g_p = us[0]
            if p:
                g_p = pltpu.roll(g_p, (cw * (0 - p)) % lanes, 1)
            for q in range(1, grp):
                v = us[q]
                if p != q:
                    v = pltpu.roll(v, (cw * (q - p)) % lanes, 1)
                g_p = jnp.where(atom == q, v, g_p)
            gps.append(g_p)
        gj = jnp.concatenate(gps, axis=0).astype(BF16)
        gl = gl + mm(rbuf[jt].reshape(2 * seqs, lanes), gj, 1, 1)
        gr = mm(lall, gj).astype(BF16)
        for h in range(2):
            grsend[h, jt] = gr[h * seqs : (h + 1) * seqs]

    for jt in range(jts):
        for h in range(2):
            owner = e * jts + jt
            here = jnp.logical_and(e == h, owner == k)

            @pl.when(here)
            def _():
                pltpu.make_async_copy(grsend.at[h, jt], grrecv.at[k], sem_gr.at[k]).start()

            @pl.when(jnp.logical_not(here))
            def _():
                rcopy(grsend.at[h, jt], grrecv.at[k], snd_gr.at[h, jt], sem_gr.at[k], h, owner).start()

    gbuf_l = jnp.where(e == 0, gl[seqs:], gl[:seqs])
    gl_own = jnp.where(e == 0, gl[:seqs], gl[seqs:])
    glsend[...] = gbuf_l
    c_gl = rcopy(glsend, glrecv, snd_gl, sem_gl, f, k)
    c_gl.start()

    d_out = mm(outer_b, opm, 0, 0).astype(BF16)
    d_mid = mm(pnormed, grad_hidden, 0, 0).astype(BF16)
    d_fin = mm(hidden, masked_grad, 0, 0).astype(BF16)
    wb[0] = d_out.reshape(ncol, rows, z)
    per = z // rows
    for b in range(d_mid.shape[1] // z):
        wb[1, b * per : (b + 1) * per] = d_mid[:, b * z : (b + 1) * z].reshape(per, rows, z)
    half = (d_mid.shape[1] // z) * per
    wb[1, half:] = d_fin.reshape(ncol - half, rows, z)
    c_w1 = rcopy(wb.at[f], w1recv, snd_w1, sem_w1, f, k)
    c_w1.start()
    c_w1.wait()
    w1s[...] = (wb[e].astype(F32) + w1recv[...].astype(F32)).astype(BF16)

    def w2_copy(t):
        kk = lax.rem(k + t, ncol)
        return rcopy(w1s.at[kk], w2recv.at[k], snd_w2.at[t], sem_w2.at[k], e, kk)

    for t in range(1, ncol):
        w2_copy(t).start()
    w2recv[k] = w1s[k]

    c_gl.wait()
    grad_l = ((gl_own + glrecv[...]) * ml).astype(BF16).astype(F32)
    for kk in range(ncol):
        rcopy(grsend.at[0, 0], grrecv.at[kk], snd_gr.at[0, 0], sem_gr.at[kk], e, k).wait_recv()

    gr_sum = grrecv[0].astype(F32)
    for kk in range(1, ncol):
        gr_sum = gr_sum + grrecv[kk].astype(F32)
    grad_r = (gr_sum * mr).astype(BF16).astype(F32)
    tw = 2 * cw
    fold_l = iota((lanes, 2 * tw), 0)
    fold_c = iota((lanes, 2 * tw), 1)
    c_of = grp * lax.div(lax.rem(fold_l, cw), res) + lax.div(fold_l, cw)
    sel_l = (c_of == lax.rem(fold_c, tw)).astype(F32).astype(BF16)
    sel_r = (lax.rem(fold_l, cw) + cw == lax.rem(fold_c, tw)).astype(F32).astype(BF16)
    gf = []
    for r in range(res):
        a = jnp.where(res_l == r, grad_l, 0.0).astype(BF16)
        b = jnp.where(res_r == r, grad_r, 0.0).astype(BF16)
        gf.append(mm(a, sel_l) + mm(b, sel_r))
    gfold = jnp.concatenate(gf, axis=0)
    low = iota(gfold.shape, 1) < tw
    ga = jnp.where(low, gfold, 0.0).astype(BF16)
    gb = jnp.where(low, 0.0, gfold).astype(BF16)
    nrm = normed_sc[...]
    ch = nrm.shape[1] // 2
    d12 = mm(nrm[:, :ch], ga, 0, 0) + mm(nrm[:, ch:], gb, 0, 0)
    sm[...] = d12.reshape(sm.shape)

    def s1_copy(t):
        peer = lax.rem(me + t, n)
        return rcopy(
            sm.at[peer], srecv.at[me], snd_s1.at[t], sem_s1.at[me],
            lax.div(peer, ncol), lax.rem(peer, ncol),
        )

    for t in range(1, n):
        s1_copy(t).start()
    srecv[me] = sm[me]

    for kk in range(ncol):

        @pl.when(k != kk)
        def _():
            rcopy(w1s.at[0], w2recv.at[kk], snd_w2.at[0], sem_w2.at[kk], e, k).wait_recv()

    acc = w2recv[0].astype(F32)
    for kk in range(1, ncol):
        acc = acc + w2recv[kk].astype(F32)
    w3[...] = acc.astype(BF16)
    wout[e, k] = acc.astype(BF16)

    def w3_copy(t):
        kk = lax.rem(k + t, ncol)
        return rcopy(w3, wout.at[e, k], snd_w3.at[t], sem_w3.at[k], e, kk)

    for t in range(1, ncol):
        w3_copy(t).start()

    def w4_copy(kk):
        return rcopy(wout.at[e, kk], wout.at[e, kk], snd_w4.at[kk], sem_w4.at[kk], f, k)

    w4_own = rcopy(w3, wout.at[e, k], snd_w4.at[k], sem_w4.at[k], f, k)
    w4_own.start()

    nn = mm(ga[:, :cw], fp_ref[...], 1, 1) + mm(ga[:, cw:tw], sp_ref[...], 1, 1)
    feat_ref[...] = standardize_adjoint(nn * ls_ref[...], scaled_sc[...], inv).astype(BF16)

    for p in range(n):

        @pl.when(me != p)
        def _():
            rcopy(sm.at[0], srecv.at[p], snd_s1.at[0], sem_s1.at[p], e, k).wait_recv()

    tot = srecv[0]
    for p in range(1, n):
        tot = tot + srecv[p]
    smine[...] = tot
    sout[me] = tot

    def s2_copy(t):
        peer = lax.rem(me + t, n)
        return rcopy(
            smine, sout.at[me], snd_s2.at[t], sem_s2.at[me],
            lax.div(peer, ncol), lax.rem(peer, ncol),
        )

    for t in range(1, n):
        s2_copy(t).start()

    for t in range(1, ncol):
        kk = lax.rem(k + t, ncol)
        rcopy(w3, wout.at[e, kk], snd_w3.at[0], sem_w3.at[kk], e, k).wait_recv()
        w4_copy(kk).start()

    for p in range(n):

        @pl.when(me != p)
        def _():
            rcopy(smine, sout.at[p], snd_s2.at[0], sem_s2.at[p], e, k).wait_recv()

    small_ref[...] = sout[...].reshape(small_ref.shape)
    for kk in range(ncol):
        rcopy(wout.at[f, kk], wout.at[f, kk], snd_w4.at[kk], sem_w4.at[kk], f, k).wait_recv()
    wsum_ref[...] = wout[...].reshape(wsum_ref.shape)

    for t in range(1, ncol):
        for c in r_copies(t):
            c.wait_send()
        w2_copy(t).wait_send()
        w3_copy(t).wait_send()

    @pl.when(own_e != e)
    def _():
        for c in r_copies(0):
            c.wait_send()

    for jt in range(jts):
        for h in range(2):

            @pl.when(jnp.logical_or(e != h, e * jts + jt != k))
            def _():
                rcopy(grsend.at[h, jt], grrecv.at[k], snd_gr.at[h, jt], sem_gr.at[k], f, k).wait_send()

    for t in range(1, n):
        s1_copy(t).wait_send()
        s2_copy(t).wait_send()
    for kk in range(ncol):
        w4_copy(kk).wait_send()


def on_device(ncol, x, am, pin, pm, pg, ls, fp, sp, ow, png, hw, bw):
    seqs, res, ch = x.shape
    cols, z = pin.shape[1:]
    cw = fp.shape[1]
    lanes = res * cw
    hid = hw.shape[1]
    jts = cols // res
    pairs = res * cols
    n = 2 * ncol
    outw = ow.shape[0]
    rows = outw // ncol
    srows = ch // 2 // n
    dma = pltpu.SemaphoreType.DMA
    vm = pltpu.VMEM
    scratch = [
        vm((2, seqs, lanes), BF16), vm((jts, 2, seqs, lanes), BF16), vm((8, lanes), F32),
        vm((2, 8, lanes), F32), vm((2, jts, 8, lanes), F32),
        vm((seqs, lanes), BF16), vm((seqs, lanes), BF16),
        vm((outw // lanes, pairs, lanes), F32), vm((lanes, lanes), BF16),
        vm((res * seqs, ch), F32), vm((res * seqs, ch), BF16),
        vm((2, jts, seqs, lanes), BF16), vm((ncol, seqs, lanes), BF16),
        vm((seqs, lanes), F32), vm((seqs, lanes), F32),
        vm((2, ncol, rows, z), BF16), vm((ncol, rows, z), BF16), vm((ncol, rows, z), BF16),
        vm((ncol, rows, z), BF16), vm((rows, z), BF16), vm((2, ncol, rows, z), BF16),
        vm((n, srows, 4 * cw), F32), vm((n, srows, 4 * cw), F32), vm((srows, 4 * cw), F32),
        vm((n, srows, 4 * cw), F32),
        dma, dma((jts, 2)), dma, dma((jts, 2)), dma((ncol,)), dma,
        dma, dma((ncol,)), dma((ncol,)), dma((ncol,)), dma((n,)), dma((n,)),
        dma, dma((ncol,)), dma, dma((ncol,)), dma((2, jts)), dma,
        dma, dma((ncol,)), dma((ncol,)), dma((ncol,)), dma((n,)), dma((n,)),
    ]
    spec = pl.BlockSpec(memory_space=pltpu.VMEM)
    feat, couple, wsum, small = pl.pallas_call(
        functools.partial(kernel, ncol, seqs, res, cols, cw),
        out_shape=(
            jax.ShapeDtypeStruct((res * seqs, ch), BF16),
            jax.ShapeDtypeStruct((pairs, z), BF16),
            jax.ShapeDtypeStruct((2 * outw, z), BF16),
            jax.ShapeDtypeStruct((ch // 2, 4 * cw), F32),
        ),
        in_specs=[spec] * 12,
        out_specs=(spec,) * 4,
        scratch_shapes=scratch,
        compiler_params=pltpu.CompilerParams(
            collective_id=0, has_side_effects=True, vmem_limit_bytes=60 << 20
        ),
    )(
        x.transpose(1, 0, 2).reshape(res * seqs, ch), am, pin.reshape(pairs, z), pm,
        pg.reshape(pairs, z), ls.reshape(1, ch), fp, sp, ow, png.reshape(1, z), hw, bw,
    )
    d1 = jnp.concatenate([small[:, :cw], small[:, 2 * cw : 3 * cw]], axis=0)
    d2 = jnp.concatenate([small[:, cw : 2 * cw], small[:, 3 * cw :]], axis=0)
    d_mid = wsum[outw : outw + hid].reshape(hid // z, z, z).transpose(1, 0, 2).reshape(z, hid)
    return (
        feat.reshape(res, seqs, ch).transpose(1, 0, 2),
        couple.reshape(res, cols, z),
        d1,
        d2,
        wsum[:outw].astype(F32),
        d_mid.astype(F32),
        wsum[outw + hid :].astype(F32),
    )


def solution(mesh):
    msa = P(("group", "depth"), "col")
    pair = P(("group", "col"), "depth")
    rep = P()
    part = P("group", None)
    return jax.shard_map(
        functools.partial(on_device, mesh.shape["col"]),
        mesh=mesh,
        in_specs=(msa, msa, pair, pair, pair) + (rep,) * 7,
        out_specs=(msa, pair, part, part, part, part, part),
        check_vma=False,
    )
```

```python
import functools

import jax
import jax.numpy as jnp
from jax import lax
from jax.experimental import pallas as pl
from jax.experimental.pallas import tpu as pltpu
from jax.sharding import PartitionSpec as P

EPS = 1e-05
F32 = jnp.float32
BF16 = jnp.bfloat16
MESH = pl.DeviceIdType.MESH


def mm(a, b, ca=1, cb=0):
    return lax.dot_general(a, b, (((ca,), (cb,)), ((), ())), preferred_element_type=F32)


def norm_pieces(v):
    center = v - jnp.mean(v, axis=-1, keepdims=True)
    inv = lax.rsqrt(jnp.mean(center * center, axis=-1, keepdims=True) + EPS)
    return center * inv, inv


def standardize_adjoint(g, scaled, inv):
    mean_g = jnp.mean(g, axis=-1, keepdims=True)
    mean_c = jnp.mean(g * scaled, axis=-1, keepdims=True)
    return inv * (g - mean_g - scaled * mean_c)


def iota(shape, axis):
    return lax.broadcasted_iota(jnp.int32, shape, axis)


def kernel(
    ncol, seqs, res, cols, cw,
    x_ref, am_ref, pin_ref, pm_ref, pg_ref, ls_ref, fp_ref, sp_ref, ow_ref, png_ref, hw_ref, bw_ref,
    feat_ref, couple_ref, wsum_ref, small_ref,
    lbuf, rbuf, mloc, mrow, mcol, lsend, rsend,
    outer, gbuf, scaled_sc, normed_sc,
    grsend, grrecv, glsend, glrecv,
    wb, w1recv, w1s, w2recv, w3, wout,
    sm, srecv, smine, sout,
    sem_l, sem_r, sem_ml, sem_mr, sem_gr, sem_gl, sem_w1, sem_w2, sem_w3, sem_w4, sem_s1, sem_s2,
    snd_l, snd_r, snd_ml, snd_mr, snd_gr, snd_gl, snd_w1, snd_w2, snd_w3, snd_w4, snd_s1, snd_s2,
):
    g = lax.axis_index("group")
    e = lax.axis_index("depth")
    k = lax.axis_index("col")
    f = 1 - e
    n = 2 * ncol
    me = e * ncol + k
    lanes = res * cw
    jts = cols // res
    grp = lanes // cw
    cts = cw // grp
    pairs = res * cols
    z = pin_ref.shape[1]

    barrier = pltpu.get_barrier_semaphore()
    for t in range(1, n):
        peer = lax.rem(me + t, n)
        pl.semaphore_signal(
            barrier, inc=1, device_id=(g, lax.div(peer, ncol), lax.rem(peer, ncol)),
            device_id_type=MESH,
        )

    def rcopy(src, dst, ssem, rsem, d, c):
        return pltpu.make_async_remote_copy(
            src_ref=src, dst_ref=dst, send_sem=ssem, recv_sem=rsem,
            device_id=(g, d, c), device_id_type=MESH,
        )

    rs_r = iota((res * seqs, res * seqs), 0)
    rs_c = iota((res * seqs, res * seqs), 1)
    by_res = (lax.rem(rs_r, seqs) * res + lax.div(rs_r, seqs) == rs_c).astype(F32).astype(BF16)
    scaled, inv = norm_pieces(mm(by_res, x_ref[...].astype(F32).reshape(res * seqs, x_ref.shape[2]).astype(BF16)))
    normed = (scaled * ls_ref[...]).astype(BF16)
    scaled_sc[...] = scaled
    normed_sc[...] = normed
    el_c = iota((cw, lanes), 0)
    el_l = iota((cw, lanes), 1)
    expand_l = (grp * lax.div(lax.rem(el_l, cw), res) + lax.div(el_l, cw) == el_c).astype(F32).astype(BF16)
    expand_r = (lax.rem(el_l, cw) == el_c).astype(F32).astype(BF16)
    wl = mm(fp_ref[...], expand_l, 0, 0).astype(BF16)
    wr = mm(sp_ref[...], expand_r, 0, 0).astype(BF16)
    pl_full = mm(normed, wl)
    pr_full = mm(normed, wr)
    ln = iota((seqs, lanes), 1)
    res_l = lax.rem(ln, res)
    res_r = lax.div(ln, cw)
    mask = am_ref[...].astype(F32).astype(BF16)
    r_at = iota((res, lanes), 0)
    l_at = iota((res, lanes), 1)
    ml = mm(mask, (lax.rem(l_at, res) == r_at).astype(F32).astype(BF16), 0, 0)
    mr = mm(mask, (lax.div(l_at, cw) == r_at).astype(F32).astype(BF16), 0, 0)
    zero = jnp.zeros((seqs, lanes), F32)
    left, right = zero, zero
    for r in range(res):
        left = jnp.where(res_l == r, pl_full[r * seqs : (r + 1) * seqs], left)
        right = jnp.where(res_r == r, pr_full[r * seqs : (r + 1) * seqs], right)
    left = (left * ml).astype(BF16)
    right = (right * mr).astype(BF16)
    lsend[...] = left
    rsend[...] = right
    lbuf[e] = left
    eye = (iota((seqs, lanes), 0) == ln).astype(F32).astype(BF16)
    grow = (iota((res, 8), 0) == iota((res, 8), 1)).astype(F32).astype(BF16)
    mt = mm(grow, mm(mask, eye).astype(BF16), 0, 0)
    mloc[...] = mt
    mrow[e] = mt
    own_e = lax.div(k, jts)
    own_jt = lax.rem(k, jts)

    pl.semaphore_wait(barrier, n - 1)

    c_left = rcopy(lsend, lbuf.at[e], snd_l, sem_l, f, k)
    c_ml = rcopy(mloc, mrow.at[e], snd_ml, sem_ml, f, k)

    def r_copies(t):
        kk = lax.rem(k + t, ncol)
        return (
            rcopy(rsend, rbuf.at[own_jt, e], snd_r.at[t], sem_r.at[own_jt, e], own_e, kk),
            rcopy(mloc, mcol.at[e, own_jt], snd_mr.at[t], sem_mr.at[own_jt, e], own_e, kk),
        )

    for t in range(1, ncol):
        for c in r_copies(t):
            c.start()

    @pl.when(own_e == e)
    def _():
        rbuf[own_jt, e] = right
        mcol[e, own_jt] = mt

    @pl.when(own_e != e)
    def _():
        for c in r_copies(0):
            c.start()

    c_left.start()
    c_ml.start()

    pgrad = pg_ref[...]
    sw_r = iota((pairs, pairs), 0)
    sw_c = iota((pairs, pairs), 1)
    swap = (lax.rem(sw_r, res) * cols + lax.div(sw_r, res) == sw_c).astype(F32).astype(BF16)
    pact = mm(swap, pin_ref[...])
    pgrad = mm(swap, pgrad)
    pick = (lax.rem(iota((pairs, res), 0), res) == iota((pairs, res), 1)).astype(F32).astype(BF16)
    prow = mm(pick, pm_ref[...].astype(F32).astype(BF16))
    pj_at = lax.div(iota((pairs, cols), 0), res) == iota((pairs, cols), 1)
    pcol = jnp.sum(jnp.where(pj_at, prow, 0.0), axis=1, keepdims=True)
    masked_grad = (pgrad * pcol).astype(BF16)
    back_prod = mm(masked_grad, bw_ref[...], 1, 1)

    c_left.wait()
    c_ml.wait()
    for jt in range(jts):
        for h in range(2):

            @pl.when(jnp.logical_or(own_e != e, jnp.logical_or(own_jt != jt, e != h)))
            def _():
                rcopy(rsend, rbuf.at[jt, h], snd_r.at[0], sem_r.at[jt, h], e, k).wait_recv()
                rcopy(mloc, mcol.at[h, jt], snd_mr.at[0], sem_mr.at[jt, h], e, k).wait_recv()

    pi = (lax.rem(iota((pairs, 8), 0), res) == iota((pairs, 8), 1)).astype(F32).astype(BF16)
    pj_r = lax.div(iota((pairs, jts * 8), 0), res)
    pj_l = iota((pairs, jts * 8), 1)
    pj = jnp.logical_and(
        lax.div(pj_r, res) == lax.div(pj_l, 8), lax.rem(pj_r, res) == lax.rem(pj_l, 8)
    ).astype(F32).astype(BF16)
    prod = jnp.zeros((pairs, lanes), F32)
    for h in range(2):
        mi = mm(pi, mrow[h].astype(BF16))
        mj = mm(pj, mcol[h].reshape(jts * 8, lanes).astype(BF16))
        prod = prod + mi * mj
    count = jnp.sum(prod, axis=1, keepdims=True)

    lall = lbuf[...].reshape(2 * seqs, lanes)
    atom = lax.div(iota((cw, lanes), 1), cw)
    top = lax.rem(iota((cw, lanes), 0), 2 * res) < res
    for jt in range(jts):
        o = mm(lall, rbuf[jt].reshape(2 * seqs, lanes), 0, 0)
        ts = []
        for q in range(grp):
            t_q = o[0:cw]
            if q:
                t_q = pltpu.roll(t_q, (cw * (0 - q)) % lanes, 1)
            for p in range(1, grp):
                v = o[p * cw : (p + 1) * cw]
                if p != q:
                    v = pltpu.roll(v, (cw * (p - q)) % lanes, 1)
                t_q = jnp.where(atom == p, v, t_q)
            ts.append(t_q)
        for q in range(0, grp, 2):
            even = jnp.where(top, ts[q], pltpu.roll(ts[q + 1], res, 0))
            odd = jnp.where(top, pltpu.roll(ts[q], cw - res, 0), ts[q + 1])
            at = (jt * res + q) * res
            for m in range(cts // 2):
                outer[2 * m, at : at + 2 * res, :] = even[m * 2 * res : (m + 1) * 2 * res]
                outer[2 * m + 1, at : at + 2 * res, :] = odd[m * 2 * res : (m + 1) * 2 * res]
    outer_b = jnp.concatenate([outer[ct].astype(BF16) for ct in range(cts)], axis=1)
    projected = mm(outer_b, ow_ref[...])

    mid_act = pact + projected / count
    pscaled, pinv = norm_pieces(mid_act)
    pnormed = (pscaled * png_ref[...]).astype(BF16)
    pre = mm(pnormed, hw_ref[...])
    sig = jax.nn.sigmoid(pre)
    hidden = (pre * sig).astype(BF16)
    grad_hidden = (back_prod * (sig * (1.0 + pre * (1.0 - sig)))).astype(BF16)
    gs = mm(grad_hidden, hw_ref[...], 1, 1) * png_ref[...]
    grad_mid = pgrad + standardize_adjoint(gs, pscaled, pinv)
    couple_ref[...] = mm(swap, grad_mid.astype(BF16), 0, 0).astype(BF16)
    opm = (grad_mid / count).astype(BF16)

    rows = wb.shape[2]
    d_out = mm(outer_b, opm, 0, 0).astype(BF16)
    d_mid = mm(pnormed, grad_hidden, 0, 0).astype(BF16)
    d_fin = mm(hidden, masked_grad, 0, 0).astype(BF16)
    wb[0] = d_out.reshape(ncol, rows, z)
    per = z // rows
    for b in range(d_mid.shape[1] // z):
        wb[1, b * per : (b + 1) * per] = d_mid[:, b * z : (b + 1) * z].reshape(per, rows, z)
    half = (d_mid.shape[1] // z) * per
    wb[1, half:] = d_fin.reshape(ncol - half, rows, z)
    c_w1 = rcopy(wb.at[f], w1recv, snd_w1, sem_w1, f, k)
    c_w1.start()

    g_out = mm(opm, ow_ref[...], 1, 1)
    tall = 2 * res
    perm_r = iota((cts * tall, cts * tall), 0)
    perm_c = iota((cts * tall, cts * tall), 1)
    perm_q = lax.div(perm_r, cw)
    perm_t = lax.div(lax.rem(perm_r, cw), res)
    perm = (perm_t * tall + perm_q * res + lax.rem(perm_r, res) == perm_c).astype(F32).astype(BF16)
    stack = jnp.concatenate(
        [
            jnp.concatenate(
                [
                    g_out[b * tall : (b + 1) * tall, ct * lanes : (ct + 1) * lanes]
                    for b in range(pairs // tall)
                ],
                axis=1,
            )
            for ct in range(cts)
        ],
        axis=0,
    )
    moved = mm(perm, stack.astype(BF16))
    gl = jnp.zeros((2 * seqs, lanes), F32)
    for jt in range(jts):
        us = []
        gps = []
        for q in range(grp):
            b = jt * (grp // 2) + q // 2
            us.append(moved[(q % 2) * cw : (q % 2 + 1) * cw, b * lanes : (b + 1) * lanes])
        for p in range(grp):
            g_p = us[0]
            if p:
                g_p = pltpu.roll(g_p, (cw * (0 - p)) % lanes, 1)
            for q in range(1, grp):
                v = us[q]
                if p != q:
                    v = pltpu.roll(v, (cw * (q - p)) % lanes, 1)
                g_p = jnp.where(atom == q, v, g_p)
            gps.append(g_p)
        gj = jnp.concatenate(gps, axis=0).astype(BF16)
        gl = gl + mm(rbuf[jt].reshape(2 * seqs, lanes), gj, 1, 1)
        gr = mm(lall, gj).astype(BF16)
        for h in range(2):
            grsend[h, jt] = gr[h * seqs : (h + 1) * seqs]

    for jt in range(jts):
        for h in range(2):
            owner = e * jts + jt
            here = jnp.logical_and(e == h, owner == k)

            @pl.when(here)
            def _():
                pltpu.make_async_copy(grsend.at[h, jt], grrecv.at[k], sem_gr.at[k]).start()

            @pl.when(jnp.logical_not(here))
            def _():
                rcopy(grsend.at[h, jt], grrecv.at[k], snd_gr.at[h, jt], sem_gr.at[k], h, owner).start()

    gbuf_l = jnp.where(e == 0, gl[seqs:], gl[:seqs])
    gl_own = jnp.where(e == 0, gl[:seqs], gl[seqs:])
    glsend[...] = gbuf_l
    c_gl = rcopy(glsend, glrecv, snd_gl, sem_gl, f, k)
    c_gl.start()


    c_w1.wait()
    w1s[...] = (wb[e].astype(F32) + w1recv[...].astype(F32)).astype(BF16)

    def w2_copy(t):
        kk = lax.rem(k + t, ncol)
        return rcopy(w1s.at[kk], w2recv.at[k], snd_w2.at[t], sem_w2.at[k], e, kk)

    for t in range(1, ncol):
        w2_copy(t).start()
    w2recv[k] = w1s[k]

    c_gl.wait()
    grad_l = ((gl_own + glrecv[...]) * ml).astype(BF16).astype(F32)
    for kk in range(ncol):
        rcopy(grsend.at[0, 0], grrecv.at[kk], snd_gr.at[0, 0], sem_gr.at[kk], e, k).wait_recv()

    gr_sum = grrecv[0].astype(F32)
    for kk in range(1, ncol):
        gr_sum = gr_sum + grrecv[kk].astype(F32)
    grad_r = (gr_sum * mr).astype(BF16).astype(F32)
    tw = 2 * cw
    fold_l = iota((lanes, tw), 0)
    fold_c = iota((lanes, tw), 1)
    c_of = grp * lax.div(lax.rem(fold_l, cw), res) + lax.div(fold_l, cw)
    sel_l = (c_of == fold_c).astype(F32).astype(BF16)
    sel_r = (lax.rem(fold_l, cw) + cw == fold_c).astype(F32).astype(BF16)
    gf = []
    for r in range(res):
        a = jnp.where(res_l == r, grad_l, 0.0).astype(BF16)
        b = jnp.where(res_r == r, grad_r, 0.0).astype(BF16)
        gf.append(mm(a, sel_l) + mm(b, sel_r))
    gfold = jnp.concatenate(gf, axis=0).astype(BF16)
    nrm = normed_sc[...]
    d12 = mm(gfold, nrm, 0, 0)
    ch = nrm.shape[1] // 2
    d12 = jnp.concatenate([d12[:, :ch], d12[:, ch:]], axis=0)
    sm[...] = d12.reshape(sm.shape)

    def s1_copy(t):
        peer = lax.rem(me + t, n)
        return rcopy(
            sm.at[peer], srecv.at[me], snd_s1.at[t], sem_s1.at[me],
            lax.div(peer, ncol), lax.rem(peer, ncol),
        )

    for t in range(1, n):
        s1_copy(t).start()
    srecv[me] = sm[me]

    for kk in range(ncol):

        @pl.when(k != kk)
        def _():
            rcopy(w1s.at[0], w2recv.at[kk], snd_w2.at[0], sem_w2.at[kk], e, k).wait_recv()

    acc = w2recv[0].astype(F32)
    for kk in range(1, ncol):
        acc = acc + w2recv[kk].astype(F32)
    w3[...] = acc.astype(BF16)
    wout[e, k] = acc.astype(BF16)

    def w3_copy(t):
        kk = lax.rem(k + t, ncol)
        return rcopy(w3, wout.at[e, k], snd_w3.at[t], sem_w3.at[k], e, kk)

    for t in range(1, ncol):
        w3_copy(t).start()

    def w4_copy(kk):
        return rcopy(wout.at[e, kk], wout.at[e, kk], snd_w4.at[kk], sem_w4.at[kk], f, k)

    w4_own = rcopy(w3, wout.at[e, k], snd_w4.at[k], sem_w4.at[k], f, k)
    w4_own.start()

    nn = mm(gfold[:, :cw], fp_ref[...]) + mm(gfold[:, cw:], sp_ref[...])
    feat = standardize_adjoint(nn * ls_ref[...], scaled_sc[...], inv).astype(BF16)
    fr = iota((res * seqs, res * seqs), 0)
    fc = iota((res * seqs, res * seqs), 1)
    by_seq = (lax.rem(fr, res) * seqs + lax.div(fr, res) == fc).astype(F32).astype(BF16)
    feat_ref[...] = mm(by_seq, feat).reshape(feat_ref.shape).astype(BF16)

    for p in range(n):

        @pl.when(me != p)
        def _():
            rcopy(sm.at[0], srecv.at[p], snd_s1.at[0], sem_s1.at[p], e, k).wait_recv()

    tot = srecv[0]
    for p in range(1, n):
        tot = tot + srecv[p]
    smine[...] = tot
    sout[me] = tot

    def s2_copy(t):
        peer = lax.rem(me + t, n)
        return rcopy(
            smine, sout.at[me], snd_s2.at[t], sem_s2.at[me],
            lax.div(peer, ncol), lax.rem(peer, ncol),
        )

    for t in range(1, n):
        s2_copy(t).start()

    for t in range(1, ncol):
        kk = lax.rem(k + t, ncol)
        rcopy(w3, wout.at[e, kk], snd_w3.at[0], sem_w3.at[kk], e, k).wait_recv()
        w4_copy(kk).start()

    for p in range(n):

        @pl.when(me != p)
        def _():
            rcopy(smine, sout.at[p], snd_s2.at[0], sem_s2.at[p], e, k).wait_recv()

    small_ref[...] = sout[...].reshape(small_ref.shape)
    for kk in range(ncol):
        rcopy(wout.at[f, kk], wout.at[f, kk], snd_w4.at[kk], sem_w4.at[kk], f, k).wait_recv()
    wsum_ref[...] = wout[...].reshape(wsum_ref.shape)

    for t in range(1, ncol):
        for c in r_copies(t):
            c.wait_send()
        w2_copy(t).wait_send()
        w3_copy(t).wait_send()

    @pl.when(own_e != e)
    def _():
        for c in r_copies(0):
            c.wait_send()

    for jt in range(jts):
        for h in range(2):

            @pl.when(jnp.logical_or(e != h, e * jts + jt != k))
            def _():
                rcopy(grsend.at[h, jt], grrecv.at[k], snd_gr.at[h, jt], sem_gr.at[k], f, k).wait_send()

    for t in range(1, n):
        s1_copy(t).wait_send()
        s2_copy(t).wait_send()
    for kk in range(ncol):
        w4_copy(kk).wait_send()


def on_device(ncol, x, am, pin, pm, pg, ls, fp, sp, ow, png, hw, bw):
    seqs, res, ch = x.shape
    cols, z = pin.shape[1:]
    cw = fp.shape[1]
    lanes = res * cw
    hid = hw.shape[1]
    jts = cols // res
    pairs = res * cols
    n = 2 * ncol
    outw = ow.shape[0]
    rows = outw // ncol
    srows = 4 * cw // n
    dma = pltpu.SemaphoreType.DMA
    vm = pltpu.VMEM
    scratch = [
        vm((2, seqs, lanes), BF16), vm((jts, 2, seqs, lanes), BF16), vm((8, lanes), F32),
        vm((2, 8, lanes), F32), vm((2, jts, 8, lanes), F32),
        vm((seqs, lanes), BF16), vm((seqs, lanes), BF16),
        vm((outw // lanes, pairs, lanes), F32), vm((lanes, lanes), BF16),
        vm((res * seqs, ch), F32), vm((res * seqs, ch), BF16),
        vm((2, jts, seqs, lanes), BF16), vm((ncol, seqs, lanes), BF16),
        vm((seqs, lanes), F32), vm((seqs, lanes), F32),
        vm((2, ncol, rows, z), BF16), vm((ncol, rows, z), BF16), vm((ncol, rows, z), BF16),
        vm((ncol, rows, z), BF16), vm((rows, z), BF16), vm((2, ncol, rows, z), BF16),
        vm((n, srows, ch // 2), F32), vm((n, srows, ch // 2), F32), vm((srows, ch // 2), F32),
        vm((n, srows, ch // 2), F32),
        dma, dma((jts, 2)), dma, dma((jts, 2)), dma((ncol,)), dma,
        dma, dma((ncol,)), dma((ncol,)), dma((ncol,)), dma((n,)), dma((n,)),
        dma, dma((ncol,)), dma, dma((ncol,)), dma((2, jts)), dma,
        dma, dma((ncol,)), dma((ncol,)), dma((ncol,)), dma((n,)), dma((n,)),
    ]
    spec = pl.BlockSpec(memory_space=pltpu.VMEM)
    feat, couple, wsum, small = pl.pallas_call(
        functools.partial(kernel, ncol, seqs, res, cols, cw),
        out_shape=(
            jax.ShapeDtypeStruct((seqs, res, ch), BF16),
            jax.ShapeDtypeStruct((pairs, z), BF16),
            jax.ShapeDtypeStruct((2 * outw, z), BF16),
            jax.ShapeDtypeStruct((4 * cw, ch // 2), F32),
        ),
        in_specs=[spec] * 12,
        out_specs=(spec,) * 4,
        scratch_shapes=scratch,
        compiler_params=pltpu.CompilerParams(
            collective_id=0, has_side_effects=True, vmem_limit_bytes=60 << 20
        ),
    )(
        x, am.T, pin.reshape(pairs, z), pm,
        pg.reshape(pairs, z), ls.reshape(1, ch), fp.T, sp.T, ow, png.reshape(1, z), hw, bw,
    )
    d1 = jnp.concatenate([small[:cw], small[2 * cw : 3 * cw]], axis=1).T
    d2 = jnp.concatenate([small[cw : 2 * cw], small[3 * cw :]], axis=1).T
    d_mid = wsum[outw : outw + hid].reshape(hid // z, z, z).transpose(1, 0, 2).reshape(z, hid)
    return (
        feat,
        couple.reshape(res, cols, z),
        d1,
        d2,
        wsum[:outw].astype(F32),
        d_mid.astype(F32),
        wsum[outw + hid :].astype(F32),
    )


def solution(mesh):
    msa = P(("group", "depth"), "col")
    pair = P(("group", "col"), "depth")
    rep = P()
    part = P("group", None)
    return jax.shard_map(
        functools.partial(on_device, mesh.shape["col"]),
        mesh=mesh,
        in_specs=(msa, msa, pair, pair, pair) + (rep,) * 7,
        out_specs=(msa, pair, part, part, part, part, part),
        check_vma=False,
    )
```
